32 devices in a mesh: groups: 2 (over y), branch: 4 (over z), leaf: 4 (over x, core).
Axes of the slice: x: 2, y: 2, z: 4, core: 2. Of those that a mesh axis runs over, the one named last changes fastest.
Arguments:
- queries: float32 [4096, 1024], P(('groups', 'branch', 'leaf')), parts along dimension 0, may hold values from -32 to 32
- leaf_keys: float32 [4096, 128], P(('groups', 'branch', 'leaf')), parts along dimension 0, may hold values from -6 to 6
- leaf_values: float32 [4096, 128], P(('groups', 'branch', 'leaf')), parts along dimension 0, may hold values from -6 to 6
- root_keys: float32 [512, 128], P(('groups', 'branch', 'leaf')), parts along dimension 0, may hold values from -12 to 12
- root_values: float32 [512, 128], P(('groups', 'branch', 'leaf')), parts along dimension 0, may hold values from -6 to 6
- branch_keys: float32 [2048, 128], P(('groups', 'branch', 'leaf')), parts along dimension 0, may hold values from -6 to 6
- branch_values: float32 [2048, 128], P(('groups', 'branch', 'leaf')), parts along dimension 0, may hold values from -6 to 6
- d_out: float32 [4096, 1024], P(('groups', 'branch', 'leaf')), parts along dimension 0, may hold values from -6 to 6
- leaf_len: int32 [32], P(('groups', 'branch', 'leaf')), parts along dimension 0, may hold values from 1 to 128, 1280 in all
- leaf_parent: int32 [32], P(('groups', 'branch', 'leaf')), parts along dimension 0, may hold values from 0 to 255
- root_cut: int32 [8], P(('groups', 'branch')), parts along dimension 0, may hold values from 128 to 256
Outputs:
- attended: float32 [4096, 1024], P(('groups', 'branch', 'leaf')), parts along dimension 0
- d_queries: float32 [4096, 1024], P(('groups', 'branch', 'leaf')), parts along dimension 0
- d_root_kv: float32 [512, 256], P(('groups', 'branch', 'leaf')), parts along dimension 0
- d_branch_kv: float32 [2048, 256], P(('groups', 'branch', 'leaf')), parts along dimension 0
- d_leaf_kv: float32 [4096, 256], P(('groups', 'branch', 'leaf')), parts along dimension 0
The draws below stay inside these ranges and needn't reach their ends.
There are 2 independent parts, one for each index of `groups`. The reference program is written for one: setup_inputs(seed, part) draws one part's arguments, and reference() takes and returns one part's arrays. A program takes and returns all parts, laid end to end along the dimension named above; each array names one. Nothing has to cross between parts.
Inputs may be any that keep to these rules, and one draw needn't show every extreme that they name: `leaf_len`: the lengths of one tree sum to 1280, and some leaf holds 128 live tokens.
All inputs are finite; a program needn't handle non-finite values. No bound on the sum of `leaf_len` on one device may be relied on, other than what follows from the above.
Results may differ from the reference program's by a relative error of at most 0.0003.
Values sent between devices are 32-bit elements; how exact they have to be, the bound alone decides.
No kernel may reach another device: no remote copies, remote signals or barrier semaphores. Data moves between devices by JAX's collectives and lax.ppermute only.
A program may use at most 64 MiB of HBM per device.

```python
import math
import jax
import jax.numpy as jnp
import numpy as np
from jax import lax

HEAD_DIM = 128
HEADS = 8
LEAF_CAP = 128
ROOT = 256
BRANCH = 256
BRANCH_ALL = 1024
LEAVES = 16
LEAF_TOTAL = 2048
N_BRANCH = 4
N_LEAF = 4


def draw_root_keys(key, part):
    noise_key = jax.random.fold_in(jax.random.fold_in(key, 11), 0)
    entries = jnp.clip(jax.random.normal(noise_key, (ROOT, HEAD_DIM), jnp.float32), -4.0, 4.0)
    return entries.astype(jnp.float32)


def draw_queries(key, part):
    noise_key = jax.random.fold_in(jax.random.fold_in(key, 23), 0)
    entries = 2.5 * jnp.clip(jax.random.normal(noise_key, (LEAF_TOTAL, HEADS, HEAD_DIM), jnp.float32), -4.0, 4.0)
    return entries.reshape(LEAF_TOTAL, HEADS * HEAD_DIM).astype(jnp.float32)


def touch_ends(drawn, own_key, low, top_value):
    longest = drawn.shape.index(max(drawn.shape))
    spots = []
    for shift in (0, 1):
        where = [jax.random.randint(jax.random.fold_in(own_key, axis), (), 0, length) for axis, length in enumerate(drawn.shape)]
        where[longest] = (where[longest] + shift) % drawn.shape[longest]
        spots.append(tuple(where))
    return drawn.at[spots[0]].set(low).at[spots[1]].set(top_value)


def level_of(stream_key, dims, cuts, low, high):
    level = 1.0
    for position, parts in cuts:
        heights = jax.random.uniform(jax.random.fold_in(jax.random.fold_in(stream_key, 6), position), (parts,), jnp.float32, low / len(cuts), high / len(cuts))
        level = level * jnp.repeat(jnp.exp(heights), dims[position] // parts).reshape((-1,) + (1,) * (len(dims) - 1 - position))
    return level


def profile(number_of, total, reach, skew):
    weights = [(1 << 20) // math.isqrt(standing ** skew) + 1 for standing in range(2, number_of + 1)]
    surplus, counts = total - reach - (number_of - 1), [1] * (number_of - 1)
    while surplus > 0:
        free = [i for i in range(number_of - 1) if counts[i] < reach]
        whole, left = sum([weights[i] for i in free]), surplus
        for i in free:
            more = min(reach - counts[i], max(1, left * weights[i] // whole), surplus)
            counts[i] = counts[i] + more
            surplus = surplus - more
    return np.array([reach] + counts)


def uneven_parts(own_key, number_of, total, limit, lean):
    if number_of == 2:
        one = jax.random.randint(own_key, (), max(1, total - limit), min(limit, total - 1) + 1)
        return jnp.stack([one, total - one])
    sizes = jnp.asarray(profile(number_of, total, limit, lean), jnp.int32)
    pairs = (number_of - 1) // 2
    giver, sink = sizes[1:1 + 2 * pairs:2], sizes[2:2 + 2 * pairs:2]
    margin = jnp.minimum(giver - 1, limit - sink)
    shifted = jax.random.randint(jax.random.fold_in(own_key, 1), (pairs,), 0, 1 << 20) % (margin + 1)
    sizes = sizes.at[1:1 + 2 * pairs:2].set(giver - shifted).at[2:2 + 2 * pairs:2].set(sink + shifted)
    return sizes[jax.random.permutation(jax.random.fold_in(own_key, 2), number_of)]


def normal_values(key, extent, scale, limit, cuts=(), kind=jnp.bfloat16):
    gain = level_of(key, extent, cuts, -0.22, 0.18) if cuts else 1.0
    values = jax.random.normal(key, extent, jnp.float32) * scale * gain
    return jnp.minimum(jnp.maximum(values, -limit), limit).astype(kind)


def setup_inputs(seed: int = 0, part: int = 0) -> dict:
    key_list = jax.random.split(jax.random.key(seed), 12)
    part_splits = jax.random.split(jax.random.fold_in(key_list[11], part), 12)
    return {
        "queries": draw_queries(jax.random.fold_in(jax.random.fold_in(key_list[11], part), 71), part),
        "leaf_keys": normal_values(part_splits[1], (LEAF_TOTAL, HEAD_DIM), 1.5, 6.0, ((0, 16),), jnp.float32),
        "leaf_values": normal_values(part_splits[2], (LEAF_TOTAL, HEAD_DIM), 1.0, 6.0, ((0, 16),), jnp.float32),
        "root_keys": draw_root_keys(jax.random.fold_in(jax.random.fold_in(key_list[11], part), 71), part),
        "root_values": normal_values(part_splits[4], (ROOT, HEAD_DIM), 1.0, 6.0, ((0, 16),), jnp.float32),
        "branch_keys": normal_values(part_splits[5], (BRANCH_ALL, HEAD_DIM), 1.0, 6.0, ((0, 16),), jnp.float32),
        "branch_values": normal_values(part_splits[6], (BRANCH_ALL, HEAD_DIM), 1.0, 6.0, ((0, 16),), jnp.float32),
        "d_out": normal_values(part_splits[7], (LEAF_TOTAL, HEADS * HEAD_DIM), 1.0, 6.0, ((0, 16),), jnp.float32),
        "leaf_len": uneven_parts(part_splits[8], LEAVES, LEAVES * (5 * LEAF_CAP // 8), LEAF_CAP, 2).astype(jnp.int32),
        "leaf_parent": touch_ends(jax.random.randint(part_splits[9], (LEAVES,), 0, BRANCH), jax.random.fold_in(part_splits[9], 1), 0, BRANCH - 1).astype(jnp.int32),
        "root_cut": touch_ends(jax.random.randint(part_splits[10], (N_BRANCH,), ROOT // 2, ROOT + 1), jax.random.fold_in(part_splits[10], 1), ROOT // 2, ROOT).astype(jnp.int32),
    }


def leaf_attention(query_heads, whole_root_keys, whole_root_values, slice_keys, slice_values, own_keys, own_values, root_limit, parent, length):
    head_dim = own_keys.shape[1]
    score_scale = 1.0 / math.sqrt(head_dim)
    highest = lax.Precision.HIGHEST
    all_keys = jnp.concatenate([whole_root_keys, slice_keys, own_keys], axis=0)
    all_values = jnp.concatenate([whole_root_values, slice_values, own_values], axis=0)
    columns = jnp.arange(all_keys.shape[0], dtype=jnp.int32)[None, :]
    positions = jnp.arange(own_keys.shape[0], dtype=jnp.int32)[:, None]
    in_root = columns < root_limit
    in_slice = (columns >= ROOT) & (columns < ROOT + BRANCH) & (columns - ROOT <= parent)
    in_leaf = (columns >= ROOT + BRANCH) & (columns - ROOT - BRANCH <= positions)
    visible = in_root | in_slice | in_leaf
    scores = jnp.einsum('thd,kd->thk', query_heads, all_keys, precision=highest) * score_scale
    scores = jnp.where(visible[:, None, :], scores, -jnp.inf)
    row_max = lax.stop_gradient(lax.optimization_barrier(jnp.max(scores, axis=-1, keepdims=True)))
    raised = jnp.exp(scores - row_max)
    weights = raised / lax.optimization_barrier(jnp.sum(raised, axis=-1, keepdims=True))
    mixture = jnp.einsum('thk,kd->thd', weights, all_values, precision=highest)
    live_rows = (positions[:, 0] < length).astype(jnp.float32)
    return mixture * live_rows[:, None, None]

def reference(queries, leaf_keys, leaf_values, root_keys, root_values, branch_keys, branch_values, d_out, leaf_len, leaf_parent, root_cut):
    query_all = queries.reshape(LEAVES, LEAF_CAP, HEADS, HEAD_DIM)
    cotangent_all = d_out.reshape(LEAVES, LEAF_CAP, HEADS, HEAD_DIM)
    own_keys_all = leaf_keys.reshape(LEAVES, LEAF_CAP, HEAD_DIM)
    own_values_all = leaf_values.reshape(LEAVES, LEAF_CAP, HEAD_DIM)

    def per_leaf(running, inputs):
        root_total, slice_total = running
        leaf_index, query_heads, own_keys, own_values, cotangent, length, parent = inputs
        slice_index = (leaf_index // N_LEAF).astype(jnp.int32)
        offset = (slice_index * BRANCH).astype(jnp.int32)
        slice_keys = lax.dynamic_slice_in_dim(branch_keys, offset, BRANCH, 0)
        slice_values = lax.dynamic_slice_in_dim(branch_values, offset, BRANCH, 0)
        root_limit = lax.dynamic_index_in_dim(root_cut, slice_index, keepdims=False)

        def forward(query_in, rootk_in, rootv_in, slicek_in, slicev_in, ownk_in, ownv_in):
            return leaf_attention(query_in, rootk_in, rootv_in, slicek_in, slicev_in, ownk_in, ownv_in, root_limit, parent, length)
        mixture, pullback = jax.vjp(forward, query_heads, root_keys, root_values, slice_keys, slice_values, own_keys, own_values)
        gradients = pullback(cotangent)
        root_total = root_total + jnp.concatenate([gradients[1], gradients[2]], axis=1)
        slice_piece = jnp.concatenate([gradients[3], gradients[4]], axis=1)
        current = lax.dynamic_slice_in_dim(slice_total, offset, BRANCH, 0)
        slice_total = lax.dynamic_update_slice_in_dim(slice_total, current + slice_piece, offset, 0)
        outputs = (mixture.reshape(LEAF_CAP, HEADS * HEAD_DIM), gradients[0].reshape(LEAF_CAP, HEADS * HEAD_DIM), jnp.concatenate([gradients[5], gradients[6]], axis=1))
        return ((root_total, slice_total), outputs)
    initial = (jnp.zeros((ROOT, 2 * HEAD_DIM), jnp.float32), jnp.zeros((BRANCH_ALL, 2 * HEAD_DIM), jnp.float32))
    leaf_ids = jnp.arange(LEAVES, dtype=jnp.int32)
    finals, stacked = lax.scan(per_leaf, initial, (leaf_ids, query_all, own_keys_all, own_values_all, cotangent_all, leaf_len, leaf_parent))
    root_total, slice_total = finals
    attended, d_queries, d_leaf = stacked
    return (attended.reshape(LEAF_TOTAL, HEADS * HEAD_DIM), d_queries.reshape(LEAF_TOTAL, HEADS * HEAD_DIM), root_total, slice_total, d_leaf.reshape(LEAF_TOTAL, 2 * HEAD_DIM))
```

```python
import math

import jax
import jax.numpy as jnp
from jax import lax
from jax.experimental import pallas as pl
from jax.experimental.pallas import tpu as pltpu
from jax.sharding import PartitionSpec as P


HEADS_PER_STEP = 2
MASKED = -1e30


def bits_of(count):
    bits = [1 << position for position in range(count.bit_length() - 1)]
    assert 1 << len(bits) == count
    return bits


def swap(value, axis, bit):
    size = lax.axis_size(axis)
    return lax.ppermute(value, axis, [(place, place ^ bit) for place in range(size)])


def split2(value):
    high = value.astype(jnp.bfloat16)
    return high, (value - high.astype(jnp.float32)).astype(jnp.bfloat16)


def split3(value):
    high = value.astype(jnp.bfloat16)
    rest = value - high.astype(jnp.float32)
    middle = rest.astype(jnp.bfloat16)
    return high, middle, (rest - middle.astype(jnp.float32)).astype(jnp.bfloat16)


def across(left, right):
    return lax.dot_general(
        left, right, (((1,), (1,)), ((), ())), preferred_element_type=jnp.float32
    )


def plain(left, right):
    return jnp.dot(left, right, preferred_element_type=jnp.float32)


def slot_tokens(shape, per_slot, own, slot_bits):
    rows = lax.broadcasted_iota(jnp.int32, shape, 0)
    shift = per_slot.bit_length() - 1
    assert 1 << shift == per_slot
    block = jnp.full(shape, 0, jnp.int32) + own
    for position, bit in enumerate(slot_bits):
        block = block ^ (((rows >> (shift + position)) & 1) * bit)
    return block * per_slot + (rows & (per_slot - 1))


def attention_kernel(
    root_bits,
    branch_bits,
    cut_ref,
    parent_ref,
    length_ref,
    q_ref,
    d_ref,
    root_ref,
    slice_ref,
    leaf_k_ref,
    leaf_v_ref,
    attended_ref,
    dq_ref,
    keep_ref,
    send_ref,
    leaf_ref,
    k_parts,
    v_parts,
    k_turned,
    v_turned,
    bias_ref,
    s_ref,
    g_ref,
    p_parts,
    ds_parts,
    q_all,
    d_all,
):
    step = pl.program_id(0)
    root_count, slice_count = root_ref.shape[0], slice_ref.shape[0]
    rows, head_dim = leaf_k_ref.shape
    key_count = root_count + slice_count + rows
    wide = HEADS_PER_STEP * rows
    scale = 1.0 / math.sqrt(head_dim)
    log2e = math.log2(math.e)

    @pl.when(step == 0)
    def _():
        n_leaf = 1 << len(branch_bits)
        leaf_place = lax.axis_index("leaf")
        own_root = lax.axis_index("branch") * n_leaf + leaf_place
        token = slot_tokens(
            (root_count, rows), root_count >> len(root_bits), own_root, root_bits
        )
        bias_ref[:root_count] = jnp.where(token < cut_ref[0], 0.0, MASKED)
        token = slot_tokens(
            (slice_count, rows), slice_count >> len(branch_bits), leaf_place, branch_bits
        )
        bias_ref[root_count : root_count + slice_count] = jnp.where(
            token <= parent_ref[0], 0.0, MASKED
        )
        key_row = lax.broadcasted_iota(jnp.int32, (rows, rows), 0)
        query_row = lax.broadcasted_iota(jnp.int32, (rows, rows), 1)
        bias_ref[root_count + slice_count :] = jnp.where(key_row <= query_row, 0.0, MASKED)
        for first in range(0, key_count, rows):
            here = slice(first, first + rows)
            if first < root_count:
                keys = root_ref[first : first + rows, :head_dim]
                values = root_ref[first : first + rows, head_dim:]
            elif first < root_count + slice_count:
                start = first - root_count
                keys = slice_ref[start : start + rows, :head_dim]
                values = slice_ref[start : start + rows, head_dim:]
            else:
                keys, values = leaf_k_ref[...], leaf_v_ref[...]
            for place, part in enumerate(split3(keys)):
                k_parts[place, here] = part
            for place, part in enumerate(split2(values)):
                v_parts[place, here] = part
            for place, part in enumerate(split2(keys.T)):
                k_turned[place * head_dim : (place + 1) * head_dim, here] = part
            for place, part in enumerate(split2(values.T)):
                v_turned[place * head_dim : (place + 1) * head_dim, here] = part

    def stacked(block):
        return jnp.concatenate(
            [
                block[:, head * head_dim : (head + 1) * head_dim]
                for head in range(HEADS_PER_STEP)
            ],
            axis=0,
        )

    def doubled(left, right):
        return jnp.concatenate([left, right], axis=1)

    lanes = pl.ds(pl.multiple_of(step * wide, wide), wide)
    q_high, q_mid, q_low = split3(stacked(q_ref[...]) * (scale * log2e))
    live = lax.broadcasted_iota(jnp.int32, (rows, 1), 0) < length_ref[0]
    d_high, d_mid = split2(stacked(jnp.where(live, d_ref[...], 0.0)))
    q_pair = doubled(q_high, q_mid)
    d_pair = doubled(d_high, d_mid)
    q_all[lanes] = q_pair
    d_all[lanes] = d_pair

    k_high, k_mid, k_low = k_parts[0], k_parts[1], k_parts[2]
    bias = bias_ref[...]
    scores = (
        across(doubled(k_high, k_high), q_pair)
        + across(doubled(k_mid, k_mid), q_pair)
        + across(doubled(k_high, k_low), doubled(q_low, q_high))
    ) + jnp.concatenate([bias] * HEADS_PER_STEP, axis=1)
    s_ref[...] = scores
    top = jnp.max(s_ref[...], axis=0, keepdims=True)
    s_ref[...] = jnp.exp2(s_ref[...] - top)
    inverse = 1.0 / jnp.sum(s_ref[...], axis=0, keepdims=True)
    s_ref[...] = s_ref[...] * inverse
    p_high, p_mid = split2(s_ref[...])
    p_parts[0, :, lanes] = p_high
    p_parts[1, :, lanes] = p_mid
    g_ref[...] = across(doubled(v_parts[0], v_parts[0]), d_pair) + across(
        doubled(v_parts[1], v_parts[1]), d_pair
    )
    row_dot = jnp.sum(s_ref[...] * g_ref[...], axis=0, keepdims=True)
    ds_high, ds_mid = split2(s_ref[...] * (g_ref[...] - row_dot))
    ds_parts[0, :, lanes] = ds_high
    ds_parts[1, :, lanes] = ds_mid

    turned = plain(v_turned[...], p_parts[0, :, lanes]) + plain(
        v_turned[...], p_parts[1, :, lanes]
    )
    turned = turned[:head_dim] + turned[head_dim:]
    dq_turned = plain(k_turned[...], ds_parts[0, :, lanes]) + plain(
        k_turned[...], ds_parts[1, :, lanes]
    )
    dq_turned = (dq_turned[:head_dim] + dq_turned[head_dim:]) * scale
    for head in range(HEADS_PER_STEP):
        here = slice(head * head_dim, (head + 1) * head_dim)
        there = slice(head * rows, (head + 1) * rows)
        attended_ref[:, here] = jnp.where(live, turned[:, there].T, 0.0)
        dq_ref[:, here] = dq_turned[:, there].T

    @pl.when(step == pl.num_programs(0) - 1)
    def _():
        def pair_grad(first, count):
            here = slice(first, first + count)
            value = plain(p_parts[0, here], d_all[...]) + plain(p_parts[1, here], d_all[...])
            key = plain(ds_parts[0, here], q_all[...]) + plain(ds_parts[1, here], q_all[...])
            return doubled(
                (key[:, :head_dim] + key[:, head_dim:]) * math.log(2.0),
                value[:, :head_dim] + value[:, head_dim:],
            )

        root_half, slice_half = root_count // 2, slice_count // 2
        keep_ref[:root_half] = pair_grad(0, root_half)
        send_ref[:root_half] = pair_grad(root_half, root_half)
        keep_ref[root_half:] = pair_grad(root_count, slice_half)
        send_ref[root_half:] = pair_grad(root_count + slice_half, slice_half)
        leaf_ref[...] = pair_grad(root_count + slice_count, rows)


def attention(root_bits, branch_bits, cut, parent, length, q, d, root, part, leaf_k, leaf_v):
    rows, width = q.shape
    head_dim = leaf_k.shape[1]
    wide = HEADS_PER_STEP * head_dim
    steps = width // wide
    root_count, slice_count = root.shape[0], part.shape[0]
    key_count = root_count + slice_count + rows
    half = (root_count + slice_count) // 2
    all_rows = width // head_dim * rows
    scalar = pl.BlockSpec(memory_space=pltpu.SMEM)
    by_head = pl.BlockSpec((rows, wide), lambda step: (0, step))

    def whole(*shape):
        return pl.BlockSpec(shape, lambda step: (0,) * len(shape))

    bf16, f32 = jnp.bfloat16, jnp.float32
    return pl.pallas_call(
        lambda *refs: attention_kernel(root_bits, branch_bits, *refs),
        grid=(steps,),
        in_specs=[
            scalar,
            scalar,
            scalar,
            by_head,
            by_head,
            whole(root_count, 2 * head_dim),
            whole(slice_count, 2 * head_dim),
            whole(rows, head_dim),
            whole(rows, head_dim),
        ],
        out_specs=[
            by_head,
            by_head,
            whole(half, 2 * head_dim),
            whole(half, 2 * head_dim),
            whole(rows, 2 * head_dim),
        ],
        out_shape=[
            jax.ShapeDtypeStruct((rows, width), f32),
            jax.ShapeDtypeStruct((rows, width), f32),
            jax.ShapeDtypeStruct((half, 2 * head_dim), f32),
            jax.ShapeDtypeStruct((half, 2 * head_dim), f32),
            jax.ShapeDtypeStruct((rows, 2 * head_dim), f32),
        ],
        scratch_shapes=[
            pltpu.VMEM((3, key_count, head_dim), bf16),
            pltpu.VMEM((2, key_count, head_dim), bf16),
            pltpu.VMEM((2 * head_dim, key_count), bf16),
            pltpu.VMEM((2 * head_dim, key_count), bf16),
            pltpu.VMEM((key_count, rows), f32),
            pltpu.VMEM((key_count, HEADS_PER_STEP * rows), f32),
            pltpu.VMEM((key_count, HEADS_PER_STEP * rows), f32),
            pltpu.VMEM((2, key_count, all_rows), bf16),
            pltpu.VMEM((2, key_count, all_rows), bf16),
            pltpu.VMEM((all_rows, 2 * head_dim), bf16),
            pltpu.VMEM((all_rows, 2 * head_dim), bf16),
        ],
        name="tree_attention",
    )(cut, parent, length, q, d, root, part, leaf_k, leaf_v)


def shards(
    queries,
    leaf_keys,
    leaf_values,
    root_keys,
    root_values,
    branch_keys,
    branch_values,
    d_out,
    leaf_len,
    leaf_parent,
    root_cut,
):
    n_leaf = lax.axis_size("leaf")
    leaf_bits = bits_of(n_leaf)
    near, far = leaf_bits[:1], leaf_bits[1:]
    z_bits = bits_of(lax.axis_size("branch"))[::-1]
    own_root = root_keys.shape[0]

    root = jnp.concatenate([root_keys, root_values], axis=1)
    part = jnp.concatenate([branch_keys, branch_values], axis=1)
    for bit in far:
        count = root.shape[0]
        both = swap(jnp.concatenate([root, part], axis=0), "leaf", bit)
        root = jnp.concatenate([root, both[:count]], axis=0)
        part = jnp.concatenate([part, both[count:]], axis=0)
    for bit in z_bits:
        root = jnp.concatenate([root, swap(root, "branch", bit)], axis=0)
    for bit in near:
        count = root.shape[0]
        both = swap(jnp.concatenate([root, part], axis=0), "leaf", bit)
        root = jnp.concatenate([root, both[:count]], axis=0)
        part = jnp.concatenate([part, both[count:]], axis=0)
    root_bits = far + [bit * n_leaf for bit in z_bits] + near
    branch_bits = far + near

    attended, d_queries, keep, send, leaf_pairs = attention(
        root_bits,
        branch_bits,
        root_cut,
        leaf_parent,
        leaf_len,
        queries,
        d_out,
        root,
        part,
        leaf_keys,
        leaf_values,
    )

    keep = keep + swap(send, "leaf", near[0])
    count = root.shape[0] // 2
    root_sum, part_sum = keep[:count], keep[count:]
    for bit in z_bits[::-1]:
        half = root_sum.shape[0] // 2
        root_sum = root_sum[:half] + swap(root_sum[half:], "branch", bit)
    for bit in far[::-1]:
        root_half, part_half = root_sum.shape[0] // 2, part_sum.shape[0] // 2
        both = swap(
            jnp.concatenate([root_sum[root_half:], part_sum[part_half:]], axis=0), "leaf", bit
        )
        root_sum = root_sum[:root_half] + both[:root_half]
        part_sum = part_sum[:part_half] + both[root_half:]
    assert root_sum.shape[0] == own_root
    return attended, d_queries, root_sum, part_sum, leaf_pairs


def solution(mesh):
    rows = P(("groups", "branch", "leaf"), None)
    numbers = P(("groups", "branch", "leaf"))
    return jax.shard_map(
        shards,
        mesh=mesh,
        in_specs=(rows,) * 8 + (numbers, numbers, P(("groups", "branch"))),
        out_specs=(rows,) * 5,
        check_vma=False,
    )
```
